768 devices in a mesh: replica: 8 (over y), fsdp: 24 (over z_lo, x), tensor: 4 (over z_hi, core).
Axes of the slice: x: 4, y: 8, z: 12 (z_hi: 2, z_lo: 6; z = z_hi * 6 + z_lo), core: 2. Of those that a mesh axis runs over, the one named last changes fastest.
Arguments:
- tokens: bfloat16 [8, 192, 4096], P('replica', ('fsdp', 'tensor')), may hold values from -6 to 6
- d_out: bfloat16 [8, 192, 4096], P('replica', ('fsdp', 'tensor')), may hold values from -6 to 6
- w_gate: bfloat16 [4096, 15360], P(None, ('fsdp', 'tensor')), may hold values from -0.09375 to 0.09375
- w_up: bfloat16 [4096, 15360], P(None, ('fsdp', 'tensor')), may hold values from -0.09375 to 0.09375
- w_down: bfloat16 [15360, 4096], P(('fsdp', 'tensor')), may hold values from -0.046875 to 0.046875
- failed: int32 [96], P(('fsdp', 'tensor')), may hold values from 0 to 7
- master: float32 [2, 15360, 4096], P(None, ('fsdp', 'tensor'), 'replica'), may hold values from -6 to 6
- moment1: float32 [2, 15360, 4096], P(None, ('fsdp', 'tensor'), 'replica'), may hold values from -4 to 4
- moment2: float32 [2, 15360, 4096], P(None, ('fsdp', 'tensor'), 'replica'), may hold values from 0.1 to 1
Outputs:
- d_tokens: bfloat16 [8, 192, 4096], P('replica', ('fsdp', 'tensor'))
- master_new: float32 [15360, 4096], P(('fsdp', 'tensor'), 'replica')
- moment1_new: float32 [15360, 4096], P(('fsdp', 'tensor'), 'replica')
- moment2_new: float32 [15360, 4096], P(('fsdp', 'tensor'), 'replica')
The draws below stay inside these ranges and needn't reach their ends.
All inputs are finite; a program needn't handle non-finite values.
Results may differ from the reference program's by a relative error of at most 0.0049.
Values may be sent and summed in bfloat16 or wider, within the bound.
A program may use at most 32 MiB of HBM per device.

```python
import math
import jax
import jax.numpy as jnp
from jax import lax

D = 4096
FF = 15360
TOK = 192
SHARDS = 96
N_REPLICA = 8
N_FSDP = 24
N_TENSOR = 4


def touch_ends(result, stream_key, low, largest):
    place = [jax.random.randint(jax.random.fold_in(stream_key, axis), (), 0, length) for axis, length in enumerate(result.shape)]
    widest = result.shape.index(max(result.shape))
    next_to = place[:widest] + [(place[widest] + 1) % result.shape[widest]] + place[widest + 1:]
    return result.at[tuple(place)].set(low).at[tuple(next_to)].set(largest)


def levels(rng, dims, split, smallest, largest):
    level = 1.0
    for position, shards_of in split:
        steps = jax.random.uniform(jax.random.fold_in(jax.random.fold_in(rng, 6), position), (shards_of,), jnp.float32, smallest / len(split), largest / len(split))
        level = level * jnp.repeat(jnp.exp(steps), dims[position] // shards_of).reshape((-1,) + (1,) * (len(dims) - 1 - position))
    return level


def bell_draw(key, shape, width, most, shards=(), held_as=jnp.bfloat16):
    drawn = jax.random.normal(key, shape, jnp.float32) * width
    if len(shards) > 0:
        drawn = levels(key, shape, shards, -0.22, 0.18) * drawn
    return jnp.clip(drawn, min=-most, max=most).astype(held_as)


def setup_inputs(seed: int = 0) -> dict:
    key_list = jax.random.split(jax.random.key(seed), 10)
    return {
        "tokens": bell_draw(key_list[0], (N_REPLICA, TOK, D), 1.0, 6.0, ((0, 8), (1, 96))),
        "d_out": bell_draw(key_list[1], (N_REPLICA, TOK, D), 1.0, 6.0, ((0, 8), (1, 96))),
        "w_gate": bell_draw(key_list[2], (D, FF), D ** -0.5, 0.09375, ((1, 96),)),
        "w_up": bell_draw(key_list[3], (D, FF), D ** -0.5, 0.09375, ((1, 96),)),
        "w_down": bell_draw(key_list[4], (FF, D), FF ** -0.5, 0.046875, ((0, 96),)),
        "failed": touch_ends(jax.random.randint(key_list[5], (SHARDS,), 0, N_REPLICA), jax.random.fold_in(key_list[5], 1), 0, N_REPLICA - 1).astype(jnp.int32),
        "master": bell_draw(key_list[6], (2, FF, D), 1.0, 6.0, ((1, 96), (2, 8)), jnp.float32),
        "moment1": bell_draw(key_list[7], (2, FF, D), 0.5, 4.0, ((1, 96), (2, 8)), jnp.float32),
        "moment2": jnp.clip(jnp.exp(math.log(1.0) - 2.3025851 * jax.random.uniform(key_list[8], (2, FF, D), jnp.float32) ** levels(key_list[8], (2, FF, D), ((1, 96), (2, 8)), -0.2, 0.2)), 0.1, 1.0),
    }


def replica_pass(w_gate, w_up, w_down, rows, grads_out):
    gate = jnp.dot(rows, w_gate, preferred_element_type=jnp.float32)
    up = jnp.dot(rows, w_up, preferred_element_type=jnp.float32)
    sig = 1.0 / (1.0 + jnp.exp(-gate))
    hidden = (gate * sig * up).astype(jnp.bfloat16)
    d_hidden = jnp.dot(grads_out, w_down.T, preferred_element_type=jnp.float32)
    d_gate = (d_hidden * up * sig * (1.0 + gate * (1.0 - sig))).astype(jnp.bfloat16)
    d_up = (d_hidden * gate * sig).astype(jnp.bfloat16)
    d_rows = jnp.dot(d_gate, w_gate.T, preferred_element_type=jnp.float32) + jnp.dot(d_up, w_up.T, preferred_element_type=jnp.float32)
    grad_down = jnp.dot(hidden.T, grads_out, preferred_element_type=jnp.float32)
    return (d_rows.astype(jnp.bfloat16), grad_down)

def recover(stack, failed_rows):
    primary = stack[0].reshape(FF, N_REPLICA, D // N_REPLICA)
    backup = stack[1].reshape(FF, N_REPLICA, D // N_REPLICA)
    rolled = jnp.roll(backup, -1, axis=1)
    select = (jnp.arange(N_REPLICA, dtype=jnp.int32)[None, :] == failed_rows[:, None])[:, :, None]
    return jnp.where(select, rolled, primary).reshape(FF, D)

def reference(tokens, d_out, w_gate, w_up, w_down, failed, master, moment1, moment2):
    failed_rows = jnp.repeat(failed, FF // (N_FSDP * N_TENSOR)).astype(jnp.int32)

    def step(total, inputs):
        rows, grads_out, index = inputs
        d_rows, grad_down = replica_pass(w_gate, w_up, w_down, rows, grads_out)
        keep = (failed_rows != index).astype(jnp.float32)[:, None]
        return (total + keep * grad_down, d_rows)
    total, d_tokens = lax.scan(step, jnp.zeros((FF, D), jnp.float32), (tokens, d_out, jnp.arange(N_REPLICA, dtype=jnp.int32)))
    grad = total / (N_REPLICA - 1.0)
    master_old = recover(master, failed_rows)
    first_old = recover(moment1, failed_rows)
    second_old = recover(moment2, failed_rows)
    first_new = 0.9 * first_old + 0.1 * grad
    second_new = 0.95 * second_old + 0.05 * grad * grad
    master_new = master_old - 0.01 * first_new / (jnp.sqrt(second_new) + 1e-08)
    return (d_tokens, master_new, first_new, second_new)
```

```python
import functools

import jax
import jax.numpy as jnp
from jax import lax
from jax.experimental import pallas as pl
from jax.experimental.pallas import tpu as pltpu
from jax.sharding import PartitionSpec as P

MESH = pl.DeviceIdType.MESH
NX, NZ, NY = 4, 12, 8
ZH = 6
OFFS = (0, 1, 2, 3, -1, -2, -3, 4, 5, 6, -4, -5)
BF = jnp.bfloat16
F32 = jnp.float32
ROWS = 192
COLS = 512
FFD = 160
HALF = 80
GROUP = ((0, 112), (112, 80))
CHAINS = ((1, 0, 4), (-1, 1, 4), (1, 1, 3), (-1, 0, 3))
CHAIN_BASE = (0, 4, 8, 11)


def slot_of(off):
    off = (off + 5) % NZ - 5
    return OFFS.index(off)


def mod(a, n):
    return lax.rem(a + 2 * n, n)


def body(
    tok, dout, failed, wg_h, wu_h, wd_h, ma_h, m1_h, m2_h,
    dt_o, grad_o, bma_o, bm1_o, bm2_o,
    stage, recv8, tile, tokg, dog, wg, wu, wd, gsc, ysend, yrecv,
    sibs, sibr, acc, xsend, xrecv, zst, zrp, zrm, zsend, zfin, ostage, orecv,
    wsem, bs, br, as_, ar, zs, zr, gxs, gxr, gcs, gcr,
    ys, yr, cs, cr, xs, xr, ps, pr, fs, fr, os_, or_,
):
    y = lax.axis_index("replica")
    f = lax.axis_index("fsdp")
    t = lax.axis_index("tensor")
    x = lax.rem(f, NX)
    z = (t // 2) * ZH + f // NX
    c = lax.rem(t, 2)

    def dev(yy, xx, zz, cc):
        return (yy, lax.rem(zz, ZH) * NX + xx, (zz // ZH) * 2 + cc)

    def zpeer(k):
        return dev(y, x, mod(z + k, NZ), c)

    def xpeer(e):
        return dev(y, mod(x + e, NX), z, c)

    def ypeer(k):
        return dev(mod(y + k, NY), x, z, c)

    def gpeer(e, d):
        return dev(y, mod(x + e, NX), z, mod(c + d, 2))

    def jof(e, d):
        return mod(x + e, NX) * 2 + mod(c + d, 2)

    sib = dev(y, x, z, 1 - c)
    me = jof(0, 0)
    started = []

    def send(src, dst, ssem, rsem, peer):
        copy = pltpu.make_async_remote_copy(
            src_ref=src, dst_ref=dst, send_sem=ssem, recv_sem=rsem,
            device_id=peer, device_id_type=MESH,
        )
        copy.start()
        started.append(copy)

    def arrived(dst, ssem, rsem, peer):
        pltpu.make_async_remote_copy(
            src_ref=dst, dst_ref=dst, send_sem=ssem, recv_sem=rsem,
            device_id=peer, device_id_type=MESH,
        ).wait_recv()

    wcopies = [
        pltpu.make_async_copy(wg_h, wg, wsem.at[0]),
        pltpu.make_async_copy(wu_h, wu, wsem.at[1]),
    ] + [
        pltpu.make_async_copy(
            wd_h.at[:, pl.ds(COLS * j, COLS)], wd.at[j], wsem.at[2 + j]
        )
        for j in range(8)
    ]
    for copy in wcopies:
        copy.start()

    group8 = [(e, d) for e in (2, 1, 3, 0) for d in (0, 1) if (e, d) != (0, 0)]
    zoffs = (3, -3, 2, -2, 1, -1)
    barrier = pltpu.get_barrier_semaphore()
    greet = [gpeer(e, d) for e, d in group8]
    greet += [zpeer(k) for k in zoffs]
    greet += [ypeer(1), ypeer(-1)]
    for peer in greet:
        pl.semaphore_signal(barrier, inc=1, device_id=peer, device_id_type=MESH)
    for j in range(8):
        cols = pl.ds(COLS * j, COLS)
        stage[j, 0] = tok[0, :, cols]
        stage[j, 1] = dout[0, :, cols]
    recv8[me] = stage[me]
    pl.semaphore_wait(barrier, len(greet))

    def rel(e, d):
        return mod_static(-e, NX) * 2 + d

    def mod_static(a, n):
        return a % n

    for e, d in group8:
        send(
            stage.at[jof(e, d)], recv8.at[me],
            as_.at[e * 2 + d], ar.at[rel(e, d)], gpeer(e, d),
        )
    for i, (src, dst) in enumerate(((ma_h, bma_o), (m1_h, bm1_o), (m2_h, bm2_o))):
        send(src.at[1], dst, bs.at[i], br.at[i], ypeer(-1))
    for e, d in group8:
        arrived(recv8.at[jof(e, d)], as_.at[e * 2 + d], ar.at[e * 2 + d], gpeer(e, d))

    gathered = (tokg, dog)
    blk = lambda s: pl.ds(16 * s, 16)
    for i, g in enumerate(gathered):
        for j in range(8):
            tile[i, 2 * j : 2 * j + 2] = recv8[j, i].astype(F32)
        g[me, 0:16] = tile[i].astype(BF)
        for k in zoffs:
            s = slot_of(-k)
            send(g.at[me, blk(0)], g.at[me, blk(s)], zs.at[i, slot_of(k)], zr.at[i, s], zpeer(k))

    def zwait(i, off):
        s = slot_of(off)
        arrived(gathered[i].at[me, blk(s)], zs.at[i, s], zr.at[i, s], zpeer(1))

    for i, g in enumerate(gathered):
        zwait(i, -3)
        for n, k in enumerate((3, 2, 1)):
            s = slot_of(-3 - k)
            send(g.at[me, blk(slot_of(-3))], g.at[me, blk(s)], zs.at[i, 7 + n], zr.at[i, s], zpeer(k))
        zwait(i, 3)
        for n, k in enumerate((-2, -1)):
            s = slot_of(3 - k)
            send(g.at[me, blk(slot_of(3))], g.at[me, blk(s)], zs.at[i, 10 + n], zr.at[i, s], zpeer(k))

    def grp(q):
        return pl.ds(*GROUP[q])

    def to_sib(i, e, q):
        g = gathered[i]
        ref = g.at[jof(e, 0), grp(q)]
        send(ref, ref, gcs.at[i, e, q], gcr.at[i, e, q], sib)

    def from_sib(i, e, q):
        g = gathered[i]
        arrived(g.at[jof(e, 1), grp(q)], gcs.at[i, e, q], gcr.at[i, e, q], sib)

    def x_out(i, q):
        g = gathered[i]
        ref = g.at[me, grp(q)]
        for e in (2, 1, 3):
            send(ref, ref, gxs.at[i, e, q], gxr.at[i, (-e) % NX, q], xpeer(e))
        to_sib(i, 0, q)

    def x_in(i, e, q):
        g = gathered[i]
        arrived(g.at[jof(e, 0), grp(q)], gxs.at[i, e, q], gxr.at[i, e, q], xpeer(e))
        to_sib(i, e, q)

    for i in range(2):
        for off in (1, -1, 2, -2):
            zwait(i, off)
        x_out(i, 0)
        for off in (4, 5, 6, -4, -5):
            zwait(i, off)
        x_out(i, 1)

    wcopies[0].wait()
    wcopies[1].wait()

    def wrows(j):
        return pl.ds(pl.multiple_of(COLS * j, COLS), COLS)

    gate = jnp.zeros((ROWS, FFD), F32)
    up = jnp.zeros((ROWS, FFD), F32)

    def gate_up(gate, up, e, d):
        j = jof(e, d)
        a = tokg[j]
        gate = gate + jnp.dot(a, wg[wrows(j), :], preferred_element_type=F32)
        up = up + jnp.dot(a, wu[wrows(j), :], preferred_element_type=F32)
        return gate, up

    gate, up = gate_up(gate, up, 0, 0)
    for q in range(2):
        from_sib(0, 0, q)
    gate, up = gate_up(gate, up, 0, 1)
    for e in (1, 3, 2):
        for q in range(2):
            x_in(0, e, q)
        gate, up = gate_up(gate, up, e, 0)
    for e in (1, 3, 2):
        for q in range(2):
            from_sib(0, e, q)
        gate, up = gate_up(gate, up, e, 1)
    sig = 1.0 / (1.0 + jnp.exp(-gate))
    hidden = gate * sig * up
    hidden_t = hidden.T.astype(BF)

    for e in (1, 3, 2):
        for q in range(2):
            x_in(1, e, q)
    for e in (0, 1, 3, 2):
        for q in range(2):
            from_sib(1, e, q)

    keep = jnp.where(failed[0] == y, 0.0, 1.0).astype(F32)

    def grad_chunk(k):
        slab = mod(y + k, NY)
        gsc[k % NY] = jnp.dot(hidden_t, dog[slab], preferred_element_type=F32) * keep

    def half(h):
        return pl.ds(HALF * h, HALF)

    def y_hop(ci, h):
        s, ab, length = CHAINS[ci]
        n = CHAIN_BASE[ci] + h
        value = gsc[(s * (length - h)) % NY, half(ab)]
        if h > 0:
            arrived(yrecv.at[n - 1], ys.at[n - 1], yr.at[n - 1], ypeer(-s))
            value = value + yrecv[n - 1].astype(F32)
        ysend[n] = value.astype(BF)
        send(ysend.at[n], yrecv.at[n], ys.at[n], yr.at[n], ypeer(s))

    def y_step(h):
        for ci in range(4):
            if h < CHAINS[ci][2]:
                y_hop(ci, h)

    for k in (4, 3, -3):
        grad_chunk(k)
    y_step(0)

    for copy in wcopies[2:]:
        copy.wait()
    dh = jnp.zeros((ROWS, FFD), F32)
    for j in range(8):
        dh = dh + lax.dot_general(
            dog[j], wd[j], (((1,), (1,)), ((), ())), preferred_element_type=F32
        )
    d_gate = (dh * up * sig * (1.0 + gate * (1.0 - sig))).astype(BF)
    d_up = (dh * gate * sig).astype(BF)
    for k in (2, -2):
        grad_chunk(k)

    nt = (((1,), (1,)), ((), ()))

    def d_rows(e, d):
        j = jof(e, d)
        return lax.dot_general(d_gate, wg[wrows(j), :], nt, preferred_element_type=F32) + lax.dot_general(
            d_up, wu[wrows(j), :], nt, preferred_element_type=F32
        )

    order = (2, 1, 3, 0)

    def x_partial(e):
        arrived(sibr.at[e], cs.at[e], cr.at[e], sib)
        total = acc[e] + sibr[e].astype(F32)
        if e == 0:
            acc[0] = total
        else:
            xsend[e - 1] = total.astype(BF)
            send(
                xsend.at[e - 1, grp(1)], xrecv.at[(-e) % NX - 1, grp(1)],
                xs.at[e, 1], xr.at[(-e) % NX, 1], xpeer(e),
            )

    for n, e in enumerate(order):
        sibs[e] = d_rows(e, 1).astype(BF)
        send(sibs.at[e], sibr.at[e], cs.at[e], cr.at[e], sib)
        acc[e] = d_rows(e, 0)
        if n > 0:
            x_partial(order[n - 1])
        if n == 1:
            y_step(1)
    x_partial(0)
    for e in (2, 1, 3):
        send(
            xsend.at[e - 1, grp(0)], xrecv.at[(-e) % NX - 1, grp(0)],
            xs.at[e, 0], xr.at[(-e) % NX, 0], xpeer(e),
        )
    for k in (1, -1, 0):
        grad_chunk(k)
    y_step(2)

    for e in (2, 1, 3):
        arrived(xrecv.at[e - 1, grp(1)], xs.at[e, 1], xr.at[e, 1], xpeer(e))
    far = acc[0, grp(1)]
    for e in (2, 1, 3):
        far = far + xrecv[e - 1, grp(1)].astype(F32)
    zst[...] = far.astype(BF)
    send(zst.at[pl.ds(0, 48)], zrp, ps.at[0], pr.at[0], zpeer(3))
    send(zst.at[pl.ds(48, 32)], zrm, ps.at[1], pr.at[1], zpeer(-3))

    for e in (2, 1, 3):
        arrived(xrecv.at[e - 1, grp(0)], xs.at[e, 0], xr.at[e, 0], xpeer(e))
    near = acc[0, grp(0)]
    for e in (2, 1, 3):
        near = near + xrecv[e - 1, grp(0)].astype(F32)
    y_step(3)
    arrived(zrp, ps.at[0], pr.at[0], zpeer(-3))
    arrived(zrm, ps.at[1], pr.at[1], zpeer(3))
    for k in (3, -3, 2, -2, 1, -1):
        s = slot_of(k)
        value = near[16 * s : 16 * s + 16]
        if k > 0:
            value = value + zrp[16 * (k - 1) : 16 * k].astype(F32)
        elif k > -3:
            value = value + zrm[16 * (-k - 1) : 16 * -k].astype(F32)
        zsend[s - 1] = value.astype(BF)
        send(zsend.at[s - 1], zfin.at[slot_of(-k) - 1], fs.at[s - 1], fr.at[slot_of(-k) - 1], zpeer(k))
    total = near[0:16]
    for k in (1, -1, 2, -2, 3, -3):
        s = slot_of(k)
        arrived(zfin.at[s - 1], fs.at[s - 1], fr.at[s - 1], zpeer(k))
        total = total + zfin[s - 1].astype(F32)
    for j in range(8):
        ostage[j] = total[2 * j : 2 * j + 2].astype(BF)
    orecv[me] = ostage[me]
    for e, d in group8:
        send(
            ostage.at[jof(e, d)], orecv.at[me],
            os_.at[e * 2 + d], or_.at[rel(e, d)], gpeer(e, d),
        )

    for ci in range(4):
        s, ab, length = CHAINS[ci]
        n = CHAIN_BASE[ci] + length - 1
        arrived(yrecv.at[n], ys.at[n], yr.at[n], ypeer(-s))
    grad_o[half(0)] = gsc[0, half(0)] + yrecv[3].astype(F32) + yrecv[13].astype(F32)
    grad_o[half(1)] = gsc[0, half(1)] + yrecv[7].astype(F32) + yrecv[10].astype(F32)

    for e, d in group8:
        arrived(orecv.at[jof(e, d)], os_.at[e * 2 + d], or_.at[e * 2 + d], gpeer(e, d))
    for j in range(8):
        dt_o[:, pl.ds(COLS * j, COLS)] = orecv[j]
    for i, dst in enumerate((bma_o, bm1_o, bm2_o)):
        arrived(dst, bs.at[i], br.at[i], ypeer(1))
    for copy in started:
        copy.wait_send()


def exchange(tokens, d_out, failed, w_gate, w_up, w_down, master, moment1, moment2):
    vm = pl.BlockSpec(memory_space=pltpu.VMEM)
    sm = pl.BlockSpec(memory_space=pltpu.SMEM)
    anyw = pl.BlockSpec(memory_space=pl.ANY)
    state = jax.ShapeDtypeStruct((FFD, COLS), F32)
    sem = pltpu.SemaphoreType.DMA
    V = pltpu.VMEM
    return pl.pallas_call(
        body,
        out_shape=(jax.ShapeDtypeStruct((2, 4096), BF), state, state, state, state),
        in_specs=[vm, vm, sm, anyw, anyw, anyw, anyw, anyw, anyw],
        out_specs=(vm, vm, anyw, anyw, anyw),
        scratch_shapes=[
            V((8, 2, 2, COLS), BF), V((8, 2, 2, COLS), BF), V((2, 16, COLS), F32),
            V((8, ROWS, COLS), BF), V((8, ROWS, COLS), BF),
            V((4096, FFD), BF), V((4096, FFD), BF), V((8, FFD, COLS), BF),
            V((8, FFD, COLS), F32), V((14, HALF, COLS), BF), V((14, HALF, COLS), BF),
            V((4, ROWS, COLS), BF), V((4, ROWS, COLS), BF), V((4, ROWS, COLS), F32),
            V((3, ROWS, COLS), BF), V((3, ROWS, COLS), BF),
            V((80, COLS), BF), V((48, COLS), BF), V((32, COLS), BF),
            V((6, 16, COLS), BF), V((6, 16, COLS), BF),
            V((8, 2, COLS), BF), V((8, 2, COLS), BF),
            sem((10,)), sem((3,)), sem((3,)), sem((8,)), sem((8,)),
            sem((2, 12)), sem((2, 12)), sem((2, 4, 2)), sem((2, 4, 2)),
            sem((2, 4, 2)), sem((2, 4, 2)),
            sem((14,)), sem((14,)), sem((4,)), sem((4,)), sem((4, 2)), sem((4, 2)),
            sem((2,)), sem((2,)), sem((6,)), sem((6,)), sem((8,)), sem((8,)),
        ],
        compiler_params=pltpu.CompilerParams(
            collective_id=0, has_side_effects=True, vmem_limit_bytes=48 << 20
        ),
        name="exchange",
    )(tokens, d_out, failed, w_gate, w_up, w_down, master, moment1, moment2)


def per_device(tokens, d_out, w_gate, w_up, w_down, failed, master, moment1, moment2):
    d_tokens, total, back0, back1, back2 = exchange(
        tokens, d_out, failed, w_gate, w_up, w_down, master, moment1, moment2
    )
    grad = total / (lax.axis_size("replica") - 1.0)
    lost = lax.axis_index("replica") == failed[0]
    master_old = jnp.where(lost, back0, master[0])
    first_old = jnp.where(lost, back1, moment1[0])
    second_old = jnp.where(lost, back2, moment2[0])
    first_new = 0.9 * first_old + 0.1 * grad
    second_new = 0.95 * second_old + 0.05 * grad * grad
    master_new = master_old - 0.01 * first_new / (jnp.sqrt(second_new) + 1e-08)
    return (d_tokens[None], master_new, first_new, second_new)


def solution(mesh):
    placed = (
        P("replica", ("fsdp", "tensor"), None),
        P("replica", ("fsdp", "tensor"), None),
        P(None, ("fsdp", "tensor")),
        P(None, ("fsdp", "tensor")),
        P(("fsdp", "tensor"), None),
        P(("fsdp", "tensor")),
        P(None, ("fsdp", "tensor"), "replica"),
        P(None, ("fsdp", "tensor"), "replica"),
        P(None, ("fsdp", "tensor"), "replica"),
    )
    return jax.shard_map(
        per_device,
        mesh=mesh,
        in_specs=placed,
        out_specs=(
            P("replica", ("fsdp", "tensor"), None),
            P(("fsdp", "tensor"), "replica"),
            P(("fsdp", "tensor"), "replica"),
            P(("fsdp", "tensor"), "replica"),
        ),
        check_vma=False,
    )
```
